32 devices in a mesh: expert: 8 (over y, x, core), place: 4 (over z).
Axes of the slice: x: 2, y: 2, z: 4, core: 2. Of those that a mesh axis runs over, the one named last changes fastest.
Arguments:
- tokens: bfloat16 [4096, 2048], P(('expert', 'place')), may hold values from -6 to 6
- out_grad: bfloat16 [4096, 2048], P(('expert', 'place')), may hold values from -6 to 6
- gate_values: float32 [4096, 8], P(('expert', 'place')), may hold values from 0.05 to 0.3
- routes: int32 [4096, 8], P(('expert', 'place')), may hold values from 0 to 31, as said below
- gate_matrix: bfloat16 [32, 2048, 768], P(('expert', 'place')), may hold values from -0.125 to 0.125
- up_matrix: bfloat16 [32, 2048, 768], P(('expert', 'place')), may hold values from -0.125 to 0.125
- down_matrix: bfloat16 [32, 768, 2048], P(('expert', 'place')), may hold values from -0.21875 to 0.21875
Outputs:
- output: float32 [4096, 2048], P(('expert', 'place'))
- gate_grad: float32 [4096, 8], P(('expert', 'place'))
- input_grad: float32 [4096, 2048], P(('expert', 'place'))
The draws below stay inside these ranges and needn't reach their ends.
Inputs may be any that keep to these rules, and one draw needn't show every extreme that they name: `routes`: each row names 8 different experts. Experts form groups of 4 consecutive numbers. In the 128 rows of one device, one expert of each group, the same one on every device, is named by more rows than any other expert of its group and by at most 64 rows; every other expert is named by at most 32 rows.
All inputs are finite; a program needn't handle non-finite values.
Results may differ from the reference program's by a relative error of at most 0.0041.
Values may be sent and summed in bfloat16 or wider, within the bound.
No kernel may reach another device: no remote copies, remote signals or barrier semaphores. Data moves between devices by JAX's collectives and lax.ppermute only.
A program may use at most 192 MiB of HBM per device.

```python
import jax
import jax.numpy as jnp
from jax import lax

D = 2048
FF = 768
TOP = 8
TOK_DEV = 128
EXPERTS = 32
COPIES = 4
MOST = 32
TOKENS = 4096


def draw_routes(key, part):
    base_key = jax.random.fold_in(key, 7)
    key_list = jax.random.split(base_key, 5)
    blocks = TOKENS // TOK_DEV
    groups = EXPERTS // COPIES
    per_dev = TOK_DEV * TOP
    hot_local = jax.random.randint(key_list[0], (groups,), 0, COPIES)
    block_ids = jnp.arange(blocks)[:, None]
    group_ids = jnp.arange(groups)[None, :]
    phase_index = (block_ids + group_ids) % 3
    drawn = jax.random.randint(key_list[1], (blocks, groups), MOST + 1, 2 * MOST + 1)
    heavy_count = jnp.where(phase_index == 0, 2 * MOST, jnp.where(phase_index == 1, MOST + 1, drawn))
    rest_count = COPIES * MOST - heavy_count
    local_index = jnp.arange(COPIES)[None, None, :]
    order_normal = (local_index - hot_local[None, :, None] - 1) % COPIES
    rotate = jax.random.randint(key_list[2], (blocks, groups, 1), 0, COPIES - 1)
    rank_normal = (order_normal + rotate) % (COPIES - 1)
    normal_count = jnp.clip(rest_count[:, :, None] - rank_normal * MOST, 0, MOST)
    counts = jnp.where(local_index == hot_local[None, :, None], heavy_count[:, :, None], normal_count).reshape(blocks, EXPERTS)
    expert_orders = jax.vmap(lambda subkey: jax.random.permutation(subkey, EXPERTS))(jax.random.split(key_list[3], blocks))
    ordered = jnp.take_along_axis(counts, expert_orders, axis=1)
    run_ends = jnp.cumsum(ordered, axis=1)
    places = jnp.arange(per_dev)
    run_index = jnp.sum((run_ends[:, None, :] <= places[None, :, None]).astype(jnp.int32), axis=2)
    listed = jnp.take_along_axis(expert_orders, run_index, axis=1)
    id_table = listed.reshape(blocks, TOP, TOK_DEV).transpose(0, 2, 1)
    row_perm = jax.vmap(lambda subkey: jax.random.permutation(subkey, TOK_DEV))(jax.random.split(key_list[4], blocks))
    id_table = jnp.take_along_axis(id_table, row_perm[:, :, None], axis=1)
    return id_table.reshape(TOKENS, TOP).astype(jnp.int32)


def block_levels(key, shape, pieces, low, high):
    def one(axis_at, shards_of):
        draws = jax.random.uniform(jax.random.fold_in(jax.random.fold_in(key, 6), axis_at), (shards_of,), jnp.float32, low / len(pieces), high / len(pieces))
        return jnp.repeat(jnp.exp(draws), shape[axis_at] // shards_of).reshape((-1,) + (1,) * (len(shape) - axis_at - 1))

    gain = one(*pieces[0])
    for cut in pieces[1:]:
        gain = gain * one(*cut)
    return gain


def noise(own_key, dims, spread, limit, shards=(), kind=jnp.bfloat16):
    values = spread * jax.random.normal(own_key, dims, jnp.float32)
    if shards:
        values = values * block_levels(own_key, dims, shards, -0.22, 0.18)
    return jnp.clip(values, -limit, limit).astype(kind)


def setup_inputs(seed: int = 0) -> dict:
    keys = jax.random.split(jax.random.key(seed), 8)
    tokens = noise(keys[0], (TOKENS, D), 1.0, 6.0, ((0, 32),))
    out_grad = noise(keys[1], (TOKENS, D), 1.0, 6.0, ((0, 32),))
    gate_values = jnp.clip(0.05 + 0.25 * jax.random.uniform(keys[2], (TOKENS, TOP), jnp.float32) ** block_levels(keys[2], (TOKENS, TOP), ((0, 32),), -0.2, 0.2), 0.05, 0.3)
    routes = draw_routes(jax.random.fold_in(keys[7], 71), 0)
    gate_matrix = noise(keys[4], (EXPERTS, D, FF), D ** -0.5, 0.125, ((0, 32),))
    up_matrix = noise(keys[5], (EXPERTS, D, FF), D ** -0.5, 0.125, ((0, 32),))
    down_matrix = noise(keys[6], (EXPERTS, FF, D), FF ** -0.5, 0.21875, ((0, 32),))
    return dict(tokens=tokens, out_grad=out_grad, gate_values=gate_values, routes=routes, gate_matrix=gate_matrix, up_matrix=up_matrix, down_matrix=down_matrix)


def pre_activations(row_block, matrices):
    gate_matrix, up_matrix, down_matrix = matrices
    gate_pre = jnp.dot(row_block, gate_matrix, preferred_element_type=jnp.float32)
    up_pre = jnp.dot(row_block, up_matrix, preferred_element_type=jnp.float32)
    return gate_pre, up_pre


def expert_forward(gate_pre, up_pre, matrices):
    hidden = (gate_pre * jax.nn.sigmoid(gate_pre) * up_pre).astype(jnp.bfloat16)
    return jnp.dot(hidden, matrices[2], preferred_element_type=jnp.float32).astype(jnp.bfloat16)


def expert_backward(gate_pre, up_pre, grad_rows, matrices):
    gate_matrix, up_matrix, down_matrix = matrices
    contract = (((1,), (1,)), ((), ()))
    hidden_grad = lax.dot_general(grad_rows, down_matrix, contract, preferred_element_type=jnp.float32)
    sigmoid_gate = jax.nn.sigmoid(gate_pre)
    gate_in = (hidden_grad * up_pre * sigmoid_gate * (1.0 + gate_pre * (1.0 - sigmoid_gate))).astype(jnp.bfloat16)
    up_in = (hidden_grad * gate_pre * sigmoid_gate).astype(jnp.bfloat16)
    back_rows = lax.dot_general(gate_in, gate_matrix, contract, preferred_element_type=jnp.float32)
    back_rows = back_rows + lax.dot_general(up_in, up_matrix, contract, preferred_element_type=jnp.float32)
    return back_rows.astype(jnp.bfloat16)


def reference(tokens, out_grad, gate_values, routes, gate_matrix, up_matrix, down_matrix):
    block_rows = 256
    assign_total = TOKENS * TOP
    assigned = routes.reshape(-1).astype(jnp.int32)
    sort_order = jnp.argsort(assigned, stable=True).astype(jnp.int32)
    counts = jnp.zeros((EXPERTS,), jnp.int32).at[assigned].add(1)
    padded = ((counts + block_rows - 1) // block_rows) * block_rows
    run_ends = jnp.cumsum(padded).astype(jnp.int32)
    starts = (run_ends - padded).astype(jnp.int32)
    firsts = (jnp.cumsum(counts) - counts).astype(jnp.int32)
    sorted_experts = assigned[sort_order]
    placed = (starts[sorted_experts] + jnp.arange(assign_total, dtype=jnp.int32) - firsts[sorted_experts]).astype(jnp.int32)
    blocks = (assign_total + EXPERTS * (block_rows - 1)) // block_rows + 1
    length = blocks * block_rows
    row_token = jnp.zeros((length,), jnp.int32).at[placed].set((sort_order // TOP).astype(jnp.int32))
    row_live = jnp.zeros((length,), jnp.int32).at[placed].set(1)
    block_first = (jnp.arange(blocks, dtype=jnp.int32) * block_rows)[:, None]
    block_expert = jnp.minimum(jnp.sum((run_ends[None, :] <= block_first).astype(jnp.int32), axis=1), EXPERTS - 1).astype(jnp.int32)

    def run_block(block_index):
        block_start = (block_index * block_rows).astype(jnp.int32)
        token_ids = lax.dynamic_slice_in_dim(row_token, block_start, block_rows)
        live_rows = lax.dynamic_slice_in_dim(row_live, block_start, block_rows)[:, None] > 0
        expert = block_expert[block_index]
        matrices = (gate_matrix[expert], up_matrix[expert], down_matrix[expert])
        row_block = jnp.where(live_rows, tokens[token_ids], jnp.zeros((), tokens.dtype))
        grad_rows = jnp.where(live_rows, out_grad[token_ids], jnp.zeros((), out_grad.dtype))
        gate_pre, up_pre = pre_activations(row_block, matrices)
        result = expert_forward(gate_pre, up_pre, matrices)
        back_rows = expert_backward(gate_pre, up_pre, grad_rows, matrices)
        return result, back_rows

    results, backs = lax.map(run_block, jnp.arange(blocks, dtype=jnp.int32))
    results = results.reshape(length, D)
    backs = backs.reshape(length, D)
    where_placed = jnp.zeros((assign_total,), jnp.int32).at[sort_order].set(placed)
    per_assign = results[where_placed].reshape(TOKENS, TOP, D).astype(jnp.float32)
    per_back = backs[where_placed].reshape(TOKENS, TOP, D).astype(jnp.float32)
    output = jnp.sum(gate_values[:, :, None] * per_assign, axis=1)
    gate_grad = jnp.sum(out_grad.astype(jnp.float32)[:, None, :] * per_assign, axis=2)
    input_grad = jnp.sum(gate_values[:, :, None] * per_back, axis=1)
    return output, gate_grad, input_grad
```

```python
import functools

import jax
import jax.numpy as jnp
from jax import lax
from jax.experimental import pallas as pl
from jax.experimental.pallas import tpu as pltpu
from jax.sharding import PartitionSpec as P


BOTH = ("expert", "place")
NT = (((1,), (1,)), ((), ()))
TN = (((0,), (0,)), ((), ()))
VMEM_LIMIT = 60 * 1024 * 1024


def column_tile(width):
    return 256 if width % 256 == 0 else width


def pack_kernel(blocks, cap, rank_ref, *refs):
    sources, (own_ref, partner_ref) = refs[:blocks], refs[blocks:]
    tokens = rank_ref.shape[-1]
    slot = lax.broadcasted_iota(jnp.int32, (cap, tokens), 0)
    for b in range(blocks):
        chosen = jnp.concatenate(
            [jnp.where(rank_ref[b, j : j + 1, :] == slot, 1.0, 0.0) for j in range(2)], axis=0
        ).astype(jnp.bfloat16)
        rows = pl.ds(b * cap, cap)
        for part in range(2):
            source = sources[b][part * tokens : (part + 1) * tokens, :]
            packed = jnp.dot(chosen, source, preferred_element_type=jnp.float32)
            packed = packed.astype(jnp.bfloat16)
            own_ref[part, rows, :] = packed[:cap]
            partner_ref[part, rows, :] = packed[cap:]


def pack(rank, sources, cap):
    blocks = len(sources)
    tokens = rank.shape[-1]
    width = sources[0].shape[1]
    tile = column_tile(width)
    out = jax.ShapeDtypeStruct((2, blocks * cap, width), jnp.bfloat16)
    return pl.pallas_call(
        functools.partial(pack_kernel, blocks, cap),
        grid=(width // tile,),
        in_specs=[pl.BlockSpec(rank.shape, lambda i: (0, 0, 0))]
        + [pl.BlockSpec((2 * tokens, tile), lambda i: (0, i))] * blocks,
        out_specs=[pl.BlockSpec((2, blocks * cap, tile), lambda i: (0, 0, i))] * 2,
        out_shape=[out, out],
        compiler_params=pltpu.CompilerParams(vmem_limit_bytes=VMEM_LIMIT),
        cost_estimate=pl.CostEstimate(
            flops=8 * blocks * cap * tokens * width,
            bytes_accessed=blocks * (tokens + 2 * cap) * width * 4,
            transcendentals=0,
        ),
        name="pack",
    )(rank, *sources)


def expert_kernel(
    rows_ref, gate_hbm, up_hbm, down_hbm, out_ref, gate_ref, up_ref, down_ref, sems
):
    copies = [
        pltpu.make_async_copy(src, dst, sems.at[k])
        for k, (src, dst) in enumerate(
            ((gate_hbm, gate_ref), (up_hbm, up_ref), (down_hbm, down_ref))
        )
    ]
    first = pl.program_id(0) == 0

    @pl.when(first)
    def _():
        for copy in copies:
            copy.start()

    def arrive(k):
        @pl.when(first)
        def _():
            copies[k].wait()

    f32 = jnp.float32
    token_rows, grad_rows = rows_ref[0], rows_ref[1]
    arrive(0)
    gate_pre = jnp.dot(token_rows, gate_ref[...], preferred_element_type=f32)
    arrive(1)
    up_pre = jnp.dot(token_rows, up_ref[...], preferred_element_type=f32)
    arrive(2)
    sig = jax.nn.sigmoid(gate_pre)
    silu = gate_pre * sig
    hidden = (silu * up_pre).astype(jnp.bfloat16)
    out_ref[0] = jnp.dot(hidden, down_ref[...], preferred_element_type=f32).astype(jnp.bfloat16)
    hidden_grad = lax.dot_general(grad_rows, down_ref[...], NT, preferred_element_type=f32)
    gate_in = (hidden_grad * up_pre * sig * (1.0 + gate_pre * (1.0 - sig))).astype(jnp.bfloat16)
    up_in = (hidden_grad * silu).astype(jnp.bfloat16)
    back = lax.dot_general(gate_in, gate_ref[...], NT, preferred_element_type=f32)
    back = back + lax.dot_general(up_in, up_ref[...], NT, preferred_element_type=f32)
    out_ref[1] = back.astype(jnp.bfloat16)


def expert(rows, weights):
    _, count, width = rows.shape
    hidden = weights[0].shape[1]
    tile = 256 if count % 256 == 0 else count
    spec = pl.BlockSpec((2, tile, width), lambda i: (0, i, 0))
    return pl.pallas_call(
        expert_kernel,
        grid=(count // tile,),
        in_specs=[spec] + [pl.BlockSpec(memory_space=pl.ANY)] * 3,
        out_specs=spec,
        out_shape=jax.ShapeDtypeStruct(rows.shape, jnp.bfloat16),
        scratch_shapes=[pltpu.VMEM(w.shape, w.dtype) for w in weights]
        + [pltpu.SemaphoreType.DMA((3,))],
        compiler_params=pltpu.CompilerParams(vmem_limit_bytes=VMEM_LIMIT),
        cost_estimate=pl.CostEstimate(
            flops=12 * count * width * hidden,
            bytes_accessed=8 * count * width + 6 * width * hidden,
            transcendentals=count * hidden,
        ),
        name="expert",
    )(rows, *weights)


def combine_kernel(blocks, cap, rank_ref, gate_ref, own_ref, other_ref, *refs):
    grads = refs[:blocks]
    outs = refs[blocks : 2 * blocks]
    dots_ref = refs[2 * blocks]
    tokens = rank_ref.shape[-1]
    slot = lax.broadcasted_iota(jnp.int32, (cap, tokens), 0)
    first = pl.program_id(0) == 0
    for b in range(blocks):
        match = [rank_ref[b, j : j + 1, :] == slot for j in range(2)]
        weight = jnp.concatenate(
            [jnp.where(match[j], gate_ref[b, j : j + 1, :], 0.0) for j in range(2)], axis=0
        )
        high = weight.astype(jnp.bfloat16)
        low = (weight - high.astype(jnp.float32)).astype(jnp.bfloat16)
        spread = jnp.concatenate([high, low], axis=0)
        rows = pl.ds(b * cap, cap)
        for part in range(2):
            held = jnp.concatenate([own_ref[part, rows, :], other_ref[part, rows, :]], axis=0)
            summed = lax.dot_general(
                spread,
                jnp.concatenate([held, held], axis=0),
                TN,
                preferred_element_type=jnp.float32,
            )
            outs[b][part * tokens : (part + 1) * tokens, :] = summed.astype(jnp.bfloat16)
            if part == 0:
                dots = lax.dot_general(held, grads[b][...], NT, preferred_element_type=jnp.float32)
                dots = jnp.concatenate(
                    [
                        jnp.sum(
                            jnp.where(match[j], dots[j * cap : (j + 1) * cap], 0.0),
                            axis=0,
                            keepdims=True,
                        )
                        for j in range(2)
                    ],
                    axis=0,
                )

                @pl.when(first)
                def _():
                    dots_ref[b] = dots

                @pl.when(jnp.logical_not(first))
                def _():
                    dots_ref[b] += dots


def combine(rank, gate, own, other, sources, cap):
    blocks = len(sources)
    tokens = rank.shape[-1]
    width = own.shape[-1]
    tile = column_tile(width)
    table = pl.BlockSpec(rank.shape, lambda i: (0, 0, 0))
    rows = pl.BlockSpec((2, blocks * cap, tile), lambda i: (0, 0, i))
    result = pl.pallas_call(
        functools.partial(combine_kernel, blocks, cap),
        grid=(width // tile,),
        in_specs=[table, table, rows, rows]
        + [pl.BlockSpec((tokens, tile), lambda i: (1, i))] * blocks,
        out_specs=[pl.BlockSpec((2 * tokens, tile), lambda i: (0, i))] * blocks + [table],
        out_shape=[jax.ShapeDtypeStruct((2 * tokens, width), jnp.bfloat16)] * blocks
        + [jax.ShapeDtypeStruct(rank.shape, jnp.float32)],
        compiler_params=pltpu.CompilerParams(vmem_limit_bytes=VMEM_LIMIT),
        cost_estimate=pl.CostEstimate(
            flops=20 * blocks * cap * tokens * width,
            bytes_accessed=blocks * (3 * tokens + 4 * cap) * width * 2,
            transcendentals=0,
        ),
        name="combine",
    )(rank, gate, own, other, *sources)
    return result[:blocks], result[blocks]


def local(tokens, out_grad, gate_values, routes, gate_matrix, up_matrix, down_matrix):
    experts = lax.axis_size("expert")
    places = lax.axis_size("place")
    devices = experts * places
    token_count, top = routes.shape
    cap = 2 * token_count * top // devices
    me = lax.axis_index("expert")
    my_place = lax.axis_index("place")
    masks = [1 << k for k in range(1, experts.bit_length() - 1)]
    evens = list(range(0, experts, 2))
    half = len(evens)

    def swap(x, mask):
        return lax.ppermute(x, "expert", [(i, i ^ mask) for i in range(experts)])

    def shift(x, step):
        if step % places == 0:
            return x
        return lax.ppermute(x, "place", [(i, (i + step) % places) for i in range(places)])

    def order_of(s):
        return masks if s % 2 == 0 else masks[::-1]

    weights = (gate_matrix[0], up_matrix[0], down_matrix[0])
    joined = jnp.concatenate([tokens, out_grad], axis=0)
    shifted = [shift(joined, s) for s in range(places)]

    by_choice = routes.T[:, None, :]
    expert_ids = jnp.arange(devices, dtype=jnp.int32)[None, :, None]
    hit = by_choice == expert_ids
    gate_map = jnp.sum(jnp.where(hit, gate_values.T[:, None, :], 0.0), axis=0)
    gate_map = jnp.where(jnp.any(hit, axis=0), gate_map, -1.0)
    gate_map = gate_map.reshape(half, 2, places, token_count)
    pair_map = jnp.stack([gate_map, gate_map[:, ::-1]], axis=3)
    pair_map = pair_map.reshape(devices, 2 * token_count)
    pair_map = lax.all_to_all(pair_map, BOTH, split_axis=0, concat_axis=0, tiled=True)
    rel_s = jnp.arange(places, dtype=jnp.int32)[:, None]
    rel_m = 2 * jnp.arange(half, dtype=jnp.int32)[None, :]
    origin = ((me ^ rel_m) * places + (my_place - rel_s) % places).reshape(-1)
    gates = pair_map[origin].reshape(places, half, 2, token_count)
    routed = gates >= 0.0
    before = jnp.arange(token_count)[:, None] < jnp.arange(token_count)[None, :]
    ranks = jnp.dot(
        routed.astype(jnp.bfloat16), before.astype(jnp.bfloat16), preferred_element_type=jnp.float32
    )
    ranks = jnp.where(routed, ranks.astype(jnp.int32), -1)

    dots = []
    totals = [None] * places
    group = 2 if places % 2 == 0 else 1
    for start in range(0, places, group):
        steps = range(start, start + group)
        sources = []
        for s in steps:
            held = {0: shifted[s]}
            for mask in order_of(s):
                held.update({k ^ mask: swap(v, mask) for k, v in held.items()})
            sources += [held[m] for m in evens]
        rank = ranks[start : start + group].reshape(-1, 2, token_count)
        gate = gates[start : start + group].reshape(-1, 2, token_count)
        own, partner = pack(rank, sources, cap)
        visiting = swap(partner, 1)
        own_result = expert(own, weights)
        partner_result = expert(visiting, weights)
        other_result = swap(partner_result, 1)
        summed, dot = combine(rank, gate, own_result, other_result, sources, cap)
        dots.append(dot)
        for j, s in enumerate(steps):
            held = dict(zip(evens, summed[j * half : (j + 1) * half]))
            for mask in order_of(s)[::-1]:
                for k in [k for k in held if k & mask]:
                    held[k ^ mask] = held[k ^ mask] + swap(held.pop(k), mask)
            totals[s] = shift(held[0], -s)

    total = sum(t.astype(jnp.float32) for t in totals)
    output, input_grad = total[:token_count], total[token_count:]

    dots = jnp.concatenate(dots, axis=0).reshape(places * half, 2 * token_count)
    to_e = jnp.arange(experts, dtype=jnp.int32)[:, None]
    to_p = jnp.arange(places, dtype=jnp.int32)[None, :]
    apart = me ^ to_e
    where_from = ((my_place - to_p) % places) * half + apart // 2
    dots = jnp.where(
        jnp.broadcast_to(apart % 2 == 0, (experts, places)).reshape(-1, 1),
        dots[where_from.reshape(-1)],
        0.0,
    )
    dots = lax.all_to_all(dots, BOTH, split_axis=0, concat_axis=0, tiled=True)
    dots = dots.reshape(half, 2, places, 2, token_count)
    dots = dots[:, :, :, 0] + dots[:, ::-1, :, 1]
    dots = dots.reshape(1, devices, token_count)
    gate_grad = jnp.sum(jnp.where(hit, dots, 0.0), axis=1).T
    return (output, gate_grad, input_grad)


def solution(mesh):
    rows = P(BOTH, None)
    matrix = P(BOTH, None, None)
    return jax.shard_map(
        local,
        mesh=mesh,
        in_specs=(rows, rows, rows, rows, matrix, matrix, matrix),
        out_specs=(rows, rows, rows),
        check_vma=False,
    )
```

```python
import functools

import jax
import jax.numpy as jnp
from jax import lax
from jax.experimental import pallas as pl
from jax.experimental.pallas import tpu as pltpu
from jax.sharding import PartitionSpec as P


BOTH = ("expert", "place")
NT = (((1,), (1,)), ((), ()))
VMEM_LIMIT = 60 * 1024 * 1024


def column_tile(width):
    return 1024 if width % 1024 == 0 else width


def pack_kernel(blocks, cap, rank_ref, *refs):
    sources, (own_ref, partner_ref) = refs[:blocks], refs[blocks:]
    tokens = rank_ref.shape[-1]
    slot = lax.broadcasted_iota(jnp.int32, (cap, tokens), 0)
    for b in range(blocks):
        chosen = jnp.concatenate(
            [jnp.where(rank_ref[0, b, j : j + 1, :] == slot, 1.0, 0.0) for j in range(2)], axis=0
        ).astype(jnp.bfloat16)
        rows = pl.ds(b * cap, cap)
        for part in range(2):
            source = sources[b][part * tokens : (part + 1) * tokens, :]
            packed = jnp.dot(chosen, source, preferred_element_type=jnp.float32)
            packed = packed.astype(jnp.bfloat16)
            own_ref[part, rows, :] = packed[:cap]
            partner_ref[part, rows, :] = packed[cap:]


def pack(s, ranks, sources, cap):
    blocks = len(sources)
    tokens = ranks.shape[-1]
    width = sources[0].shape[1]
    tile = column_tile(width)
    out = jax.ShapeDtypeStruct((2, blocks * cap, width), jnp.bfloat16)
    return pl.pallas_call(
        functools.partial(pack_kernel, blocks, cap),
        grid=(width // tile,),
        in_specs=[pl.BlockSpec((1,) + ranks.shape[1:], lambda i: (s, 0, 0, 0))]
        + [pl.BlockSpec((2 * tokens, tile), lambda i: (0, i))] * blocks,
        out_specs=[pl.BlockSpec((2, blocks * cap, tile), lambda i: (0, 0, i))] * 2,
        out_shape=[out, out],
        compiler_params=pltpu.CompilerParams(vmem_limit_bytes=VMEM_LIMIT),
        cost_estimate=pl.CostEstimate(
            flops=8 * blocks * cap * tokens * width,
            bytes_accessed=blocks * (tokens + 2 * cap) * width * 4,
            transcendentals=0,
        ),
        name="pack",
    )(ranks, *sources)


def expert_kernel(
    steps,
    own_ref,
    visit_ref,
    gate_hbm,
    up_hbm,
    down_hbm,
    own_out,
    visit_out,
    gate_ref,
    up_ref,
    down_ref,
    sems,
):
    copies = [
        pltpu.make_async_copy(src, dst, sems.at[k])
        for k, (src, dst) in enumerate(
            ((gate_hbm, gate_ref), (up_hbm, up_ref), (down_hbm, down_ref))
        )
    ]
    step = pl.program_id(0)

    @pl.when(step == 0)
    def _():
        for copy in copies:
            copy.start()

    def arrive(k):
        @pl.when(step == 0)
        def _():
            copies[k].wait()

    f32 = jnp.float32
    mine = step < steps
    token_rows = jnp.where(mine, own_ref[0], visit_ref[0])
    grad_rows = jnp.where(mine, own_ref[1], visit_ref[1])
    arrive(0)
    gate_pre = jnp.dot(token_rows, gate_ref[...], preferred_element_type=f32)
    arrive(1)
    up_pre = jnp.dot(token_rows, up_ref[...], preferred_element_type=f32)
    arrive(2)
    hidden_grad = lax.dot_general(grad_rows, down_ref[...], NT, preferred_element_type=f32)
    sig = jax.nn.sigmoid(gate_pre)
    silu = gate_pre * sig
    hidden = (silu * up_pre).astype(jnp.bfloat16)
    gate_in = (hidden_grad * up_pre * sig * (1.0 + gate_pre * (1.0 - sig))).astype(jnp.bfloat16)
    up_in = (hidden_grad * silu).astype(jnp.bfloat16)
    ahead = jnp.dot(hidden, down_ref[...], preferred_element_type=f32).astype(jnp.bfloat16)
    back = lax.dot_general(gate_in, gate_ref[...], NT, preferred_element_type=f32)
    back = back + lax.dot_general(up_in, up_ref[...], NT, preferred_element_type=f32)
    back = back.astype(jnp.bfloat16)

    @pl.when(mine)
    def _():
        own_out[0] = ahead
        own_out[1] = back

    @pl.when(jnp.logical_not(mine))
    def _():
        visit_out[0] = ahead
        visit_out[1] = back


def expert(own, visiting, weights):
    _, count, width = own.shape
    hidden = weights[0].shape[1]
    tile = 256 if count % 256 == 0 else count
    steps = count // tile
    own_spec = pl.BlockSpec((2, tile, width), lambda i: (0, jnp.minimum(i, steps - 1), 0))
    visit_spec = pl.BlockSpec((2, tile, width), lambda i: (0, jnp.maximum(i - steps, 0), 0))
    shape = jax.ShapeDtypeStruct(own.shape, jnp.bfloat16)
    return pl.pallas_call(
        functools.partial(expert_kernel, steps),
        grid=(2 * steps,),
        in_specs=[own_spec, visit_spec] + [pl.BlockSpec(memory_space=pl.ANY)] * 3,
        out_specs=[own_spec, visit_spec],
        out_shape=[shape, shape],
        scratch_shapes=[pltpu.VMEM(w.shape, w.dtype) for w in weights]
        + [pltpu.SemaphoreType.DMA((3,))],
        compiler_params=pltpu.CompilerParams(vmem_limit_bytes=VMEM_LIMIT),
        cost_estimate=pl.CostEstimate(
            flops=24 * count * width * hidden,
            bytes_accessed=16 * count * width + 6 * width * hidden,
            transcendentals=2 * count * hidden,
        ),
        name="expert",
    )(own, visiting, *weights)


def combine_kernel(blocks, cap, rank_ref, gate_ref, own_ref, other_ref, *refs):
    grads = refs[:blocks]
    ahead, back = refs[blocks : 2 * blocks], refs[2 * blocks : 3 * blocks]
    dots_ref, spread_ref = refs[3 * blocks], refs[3 * blocks + 1]
    tokens = rank_ref.shape[-1]
    slot = lax.broadcasted_iota(jnp.int32, (cap, tokens), 0)

    @pl.when(pl.program_id(0) == 0)
    def _():
        for b in range(blocks):
            weight = jnp.concatenate(
                [
                    jnp.where(
                        rank_ref[0, b, j : j + 1, :] == slot, gate_ref[0, b, j : j + 1, :], 0.0
                    )
                    for j in range(2)
                ],
                axis=0,
            ).T
            high = weight.astype(jnp.bfloat16)
            low = (weight - high.astype(jnp.float32)).astype(jnp.bfloat16)
            spread_ref[b] = jnp.concatenate([high, low], axis=1)
            dots_ref[b] = jnp.zeros_like(dots_ref[b])

    for b in range(blocks):
        rows = pl.ds(b * cap, cap)
        for part, outs in enumerate((ahead, back)):
            held = jnp.concatenate([own_ref[part, rows, :], other_ref[part, rows, :]], axis=0)
            summed = jnp.dot(
                spread_ref[b],
                jnp.concatenate([held, held], axis=0),
                preferred_element_type=jnp.float32,
            )
            outs[b][...] = summed.astype(jnp.bfloat16)
            if part == 0:
                dots = lax.dot_general(held, grads[b][...], NT, preferred_element_type=jnp.float32)
                dots_ref[b] += jnp.concatenate(
                    [
                        jnp.sum(
                            jnp.where(
                                rank_ref[0, b, j : j + 1, :] == slot,
                                dots[j * cap : (j + 1) * cap],
                                0.0,
                            ),
                            axis=0,
                            keepdims=True,
                        )
                        for j in range(2)
                    ],
                    axis=0,
                )


def combine(s, ranks, gates, own, other, sources, cap):
    blocks = len(sources)
    tokens = ranks.shape[-1]
    width = own.shape[-1]
    tile = column_tile(width)
    table = pl.BlockSpec((1,) + ranks.shape[1:], lambda i: (s, 0, 0, 0))
    rows = pl.BlockSpec((2, blocks * cap, tile), lambda i: (0, 0, i))
    result = pl.pallas_call(
        functools.partial(combine_kernel, blocks, cap),
        grid=(width // tile,),
        in_specs=[table, table, rows, rows]
        + [pl.BlockSpec((tokens, tile), lambda i: (1, i))] * blocks,
        out_specs=[pl.BlockSpec((tokens, tile), lambda i: (0, i))] * (2 * blocks)
        + [pl.BlockSpec(ranks.shape[1:], lambda i: (0, 0, 0))],
        out_shape=[jax.ShapeDtypeStruct((tokens, width), jnp.bfloat16)] * (2 * blocks)
        + [jax.ShapeDtypeStruct(ranks.shape[1:], jnp.float32)],
        scratch_shapes=[pltpu.VMEM((blocks, tokens, 4 * cap), jnp.bfloat16)],
        compiler_params=pltpu.CompilerParams(vmem_limit_bytes=VMEM_LIMIT),
        cost_estimate=pl.CostEstimate(
            flops=20 * blocks * cap * tokens * width,
            bytes_accessed=blocks * (3 * tokens + 4 * cap) * width * 2,
            transcendentals=0,
        ),
        name="combine",
    )(ranks, gates, own, other, *sources)
    return result[:blocks], result[blocks : 2 * blocks], result[2 * blocks]


def layer(tokens, out_grad, gate_values, routes, gate_matrix, up_matrix, down_matrix):
    experts = lax.axis_size("expert")
    places = lax.axis_size("place")
    devices = experts * places
    token_count, top = routes.shape
    cap = 2 * token_count * top // devices
    me = lax.axis_index("expert")
    my_place = lax.axis_index("place")
    masks = [1 << k for k in range(1, experts.bit_length() - 1)]
    evens = list(range(0, experts, 2))
    half = len(evens)

    def swap(x, mask):
        return lax.ppermute(x, "expert", [(i, i ^ mask) for i in range(experts)])

    def shift(x, step):
        if step % places == 0:
            return x
        return lax.ppermute(x, "place", [(i, (i + step) % places) for i in range(places)])

    def order_of(s):
        return masks if s % 2 == 0 else masks[::-1]

    weights = (gate_matrix[0], up_matrix[0], down_matrix[0])
    joined = jnp.concatenate([tokens, out_grad], axis=0)
    shifted = []
    for s in range(places):
        shifted.append(shift(joined, s))

    by_choice = routes.T[:, None, :]
    expert_ids = jnp.arange(devices, dtype=jnp.int32)[None, :, None]
    hit = by_choice == expert_ids
    gate_map = jnp.sum(jnp.where(hit, gate_values.T[:, None, :], 0.0), axis=0)
    gate_map = jnp.where(jnp.any(hit, axis=0), gate_map, -1.0)
    gate_map = gate_map.reshape(half, 2, places, token_count)
    pair_map = jnp.stack([gate_map, gate_map[:, ::-1]], axis=3)
    pair_map = pair_map.reshape(devices, 2 * token_count)
    pair_map = lax.all_to_all(pair_map, BOTH, split_axis=0, concat_axis=0, tiled=True)
    rel_s = jnp.arange(places, dtype=jnp.int32)[:, None]
    rel_m = 2 * jnp.arange(half, dtype=jnp.int32)[None, :]
    origin = ((me ^ rel_m) * places + (my_place - rel_s) % places).reshape(-1)
    gates = pair_map[origin].reshape(places, half, 2, token_count)
    routed = gates >= 0.0
    before = jnp.arange(token_count)[:, None] < jnp.arange(token_count)[None, :]
    ranks = jnp.dot(
        routed.astype(jnp.bfloat16), before.astype(jnp.bfloat16), preferred_element_type=jnp.float32
    )
    ranks = jnp.where(routed, ranks.astype(jnp.int32), -1)

    dots = []
    totals = []
    for s in range(places):
        held = {0: shifted[s]}
        for mask in order_of(s):
            arrived = {}
            for k, v in held.items():
                arrived[k ^ mask] = swap(v, mask)
            held.update(arrived)
        sources = [held[m] for m in evens]
        own, partner = pack(s, ranks, sources, cap)
        visiting = swap(partner, 1)
        own_result, partner_result = expert(own, visiting, weights)
        other_result = swap(partner_result, 1)
        ahead, back, dot = combine(s, ranks, gates, own_result, other_result, sources, cap)
        dots.append(dot)
        returned = []
        for blocks, order in ((ahead, masks), (back, masks[::-1])):
            held = dict(zip(evens, blocks))
            for mask in order:
                for k in [k for k in held if k & mask]:
                    arrived = swap(held.pop(k), mask)
                    held[k ^ mask] = held[k ^ mask] + arrived
            returned.append(shift(held[0], -s))
        totals.append(returned)

    output = sum(t[0].astype(jnp.float32) for t in totals)
    input_grad = sum(t[1].astype(jnp.float32) for t in totals)

    dots = jnp.concatenate(dots, axis=0).reshape(places * half, 2 * token_count)
    to_e = jnp.arange(experts, dtype=jnp.int32)[:, None]
    to_p = jnp.arange(places, dtype=jnp.int32)[None, :]
    apart = me ^ to_e
    where_from = ((my_place - to_p) % places) * half + apart // 2
    dots = jnp.where(
        jnp.broadcast_to(apart % 2 == 0, (experts, places)).reshape(-1, 1),
        dots[where_from.reshape(-1)],
        0.0,
    )
    dots = lax.all_to_all(dots, BOTH, split_axis=0, concat_axis=0, tiled=True)
    dots = dots.reshape(half, 2, places, 2, token_count)
    dots = dots[:, :, :, 0] + dots[:, ::-1, :, 1]
    dots = dots.reshape(1, devices, token_count)
    gate_grad = jnp.sum(jnp.where(hit, dots, 0.0), axis=1).T
    return (output, gate_grad, input_grad)


def solution(mesh):
    rows = P(BOTH, None)
    matrix = P(BOTH, None, None)
    return jax.shard_map(
        layer,
        mesh=mesh,
        in_specs=(rows, rows, rows, rows, matrix, matrix, matrix),
        out_specs=(rows, rows, rows),
        check_vma=False,
    )
```
